32 devices in a mesh: cuts: 4 (over x, core), fiber: 8 (over z, y).
Axes of the slice: x: 2, y: 2, z: 4, core: 2. Of those that a mesh axis runs over, the one named last changes fastest.
Arguments:
- tile_vals: bfloat16 [131072, 128], P(('cuts', 'fiber')), may hold values from -6 to 6
- tile_count: int32 [131072], P(('cuts', 'fiber')), may hold values from 1 to 128
- tile_dest: int32 [131072, 1], P(('cuts', 'fiber')), may hold values from 0 to 3; in each aligned block of 4096 rows (0 to 4095, 4096 to 8191, ...) at most 2048 rows name the same one
- tile_row: int32 [131072], P(('cuts', 'fiber')), may hold values from 0 to 1023, as said below
- tile_block: int32 [131072], P(('cuts', 'fiber')), may hold values from 0 to 3
- tile_first: int32 [131072], P(('cuts', 'fiber')), may hold values from 0 to 255
- factor_one: bfloat16 [8192, 32], P(('cuts', 'fiber')), may hold values from -1.5 to 1.5
- factor_three: bfloat16 [4096, 32], P('fiber'), may hold values from -0.5 to 0.5
- factor_two: bfloat16 [4096, 32], P(('cuts', 'fiber')), may hold values from -0.09375 to 0.09375
Outputs:
- ttmc: bfloat16 [4096, 1024], P(('cuts', 'fiber'))
- projected: float32 [4096, 32], P(('cuts', 'fiber'))
The draws below stay inside these ranges and needn't reach their ends.
Inputs may be any that keep to these rules, and one draw needn't show every extreme that they name: `tile_dest`: among the tiles of one device, each index of cuts is named at most 2048 times, and exactly 2048 times by some. `tile_row`: among the tiles of one device, each block of 128 consecutive values (starting at multiples of 128) is taken exactly 512 times.
All inputs are finite; a program needn't handle non-finite values.
Results may differ from the reference program's by a relative error of at most 0.002.
Values may be sent and summed in bfloat16 or wider, within the bound.
A program may use at most 128 MiB of HBM per device.

```python
import math
import jax
import jax.numpy as jnp
import numpy as np
from jax import lax

R1 = 32
R2 = 32
R3 = 32
FIBER = 128
TILE_DEV = 4096
I2_DEV = 1024
I1_DEV = 256
KB_DEV = 4
CAP = 2048
ROWBLK = 128
TILES = 131072
I1 = 8192
I2 = 4096
I3 = 4096
N_CUTS = 4
N_FIBER = 8


def draw_tile_row(key, part):
    devices = TILES // TILE_DEV
    device_keys = jax.random.split(jax.random.fold_in(key, 7), devices)
    shuffled = jax.vmap(lambda single: jax.random.permutation(single, TILE_DEV))(device_keys)
    row_owner = shuffled % (I2_DEV // ROWBLK)
    within = jax.random.randint(jax.random.fold_in(key, 11), (devices, TILE_DEV), 0, ROWBLK)
    return (row_owner * ROWBLK + within).reshape(TILES).astype(jnp.int32)


def plant(result, key, smallest, largest):
    extent = result.shape
    spot = [jax.random.randint(jax.random.fold_in(key, axis), (), 0, extent[axis]) for axis in range(len(extent))]
    result = result.at[tuple(spot)].set(smallest)
    longest = extent.index(max(extent))
    spot[longest] = (spot[longest] + 1) % extent[longest]
    return result.at[tuple(spot)].set(largest)


def level_of(key, shape, cuts, least, largest):
    loudness = 1.0
    for position, parts in cuts:
        heights = jax.random.uniform(jax.random.fold_in(jax.random.fold_in(key, 6), position), (parts,), jnp.float32, least / len(cuts), largest / len(cuts))
        loudness = loudness * jnp.repeat(jnp.exp(heights), shape[position] // parts).reshape((-1,) + (1,) * (len(shape) - 1 - position))
    return loudness


def shared_out(stream_key, own, number, rows, number_of, top, reach, slope):
    ranking = jax.random.permutation(stream_key, number_of)
    packed, usual = portions_of(number_of, rows * top, reach, slope, True), portions_of(number_of, rows * top, reach, slope, False)
    places = jnp.arange(number_of)

    def named(lengths, offset_by):
        used = int((lengths > 0).sum())
        fixed = max(1, used // 4)
        passed = fixed + (places - fixed + offset_by * (used - fixed)) % max(1, number_of - fixed)
        return jnp.zeros((number_of,), jnp.int32).at[ranking[jnp.where(places < fixed, places, passed)]].set(jnp.asarray(lengths, jnp.int32))

    lengths = jnp.where(number % 4 == 0, named(packed, number // 4), named(usual, number - number // 4 - 1))
    mixed = jax.random.permutation(jax.random.fold_in(own, 3), number_of)
    donor, sink = mixed[0:number_of // 2 * 2:2], mixed[1:number_of // 2 * 2:2]
    margin = jnp.minimum(lengths[donor] - 1, reach - lengths[sink]) // 2
    margin = jnp.where((donor == ranking[0]) | (sink == ranking[0]) | (lengths[sink] == 0), 0, jnp.maximum(margin, 0))
    passed = jax.random.randint(jax.random.fold_in(own, 4), (number_of // 2,), 0, 1 << 20) % (margin + 1)
    lengths = lengths.at[donor].add(-passed).at[sink].add(passed)
    labels = jnp.searchsorted(jnp.cumsum(lengths), jnp.arange(rows * top), side="right").astype(jnp.int32)
    table = labels.reshape(top, rows).T
    table = table[jax.random.permutation(jax.random.fold_in(own, 1), rows)]
    offset_by = jax.random.randint(jax.random.fold_in(own, 2), (rows, 1), 0, top)
    return jnp.take_along_axis(table, (jnp.arange(top)[None, :] + offset_by) % top, axis=1)


def portions_of(count, total, limit, slope, full):
    loads = [(1 << 20) // math.isqrt(grade ** slope) + 1 for grade in range(1, count + 1)]
    largest = limit if full else min(limit, max(-(-total // count), total * loads[0] // sum(loads)))
    least = 1 if total - largest >= count - 1 else 0
    given, spare = [largest] + [least] * (count - 1), total - largest - least * (count - 1)
    while spare > 0:
        movable = [i for i in range(1, count) if given[i] < largest] or [i for i in range(1, count) if given[i] < limit]
        whole, left = sum([loads[i] for i in movable]), spare
        for i in movable:
            more = min(limit - given[i], max(1, left * loads[i] // whole), spare)
            given[i] = given[i] + more
            spare = spare - more
    return np.array(given)


def centred(own_key, dims, deviation, limit, cuts=(), held_as=jnp.bfloat16):
    gain = level_of(own_key, dims, cuts, -0.22, 0.18) if cuts else 1.0
    drawn = jax.random.normal(own_key, dims, jnp.float32) * deviation * gain
    return jnp.minimum(jnp.maximum(drawn, -limit), limit).astype(held_as)


def setup_inputs(seed: int = 0) -> dict:
    key_of = jax.random.split(jax.random.key(seed), 10)
    tile_vals = centred(key_of[0], (TILES, FIBER), 1.0, 6.0, ((0, 32),))
    tile_count = plant(jax.random.randint(key_of[1], (TILES,), 1, FIBER + 1), jax.random.fold_in(key_of[1], 1), 1, FIBER).astype(jnp.int32)
    tile_dest_keys = jax.random.split(jax.random.fold_in(key_of[2], 1), TILES // TILE_DEV)
    tile_dest_turns = jax.random.permutation(jax.random.fold_in(key_of[2], 3), TILES // TILE_DEV)
    tile_dest = jax.vmap(lambda own, number: shared_out(jax.random.fold_in(key_of[2], 2), own, number, TILE_DEV, N_CUTS, 1, CAP, 2))(tile_dest_keys, tile_dest_turns).reshape((TILES, 1))
    tile_row = draw_tile_row(jax.random.fold_in(key_of[9], 71), 0)
    tile_block = plant(jax.random.randint(key_of[4], (TILES,), 0, KB_DEV), jax.random.fold_in(key_of[4], 1), 0, KB_DEV - 1).astype(jnp.int32)
    tile_first = plant(jax.random.randint(key_of[5], (TILES,), 0, I1_DEV), jax.random.fold_in(key_of[5], 1), 0, I1_DEV - 1).astype(jnp.int32)
    factor_one = centred(key_of[6], (I1, R1), 0.25, 1.5, ((0, 32),))
    factor_three = centred(key_of[7], (I3, R3), FIBER ** -0.5, 0.5, ((0, 8),))
    factor_two = centred(key_of[8], (I2, R2), I2 ** -0.5, 0.09375, ((0, 32),))
    return {"tile_vals": tile_vals, "tile_count": tile_count, "tile_dest": tile_dest, "tile_row": tile_row, "tile_block": tile_block, "tile_first": tile_first, "factor_one": factor_one, "factor_three": factor_three, "factor_two": factor_two}


def reference(tile_vals, tile_count, tile_dest, tile_row, tile_block, tile_first, factor_one, factor_three, factor_two):
    positions = jnp.arange(FIBER, dtype=jnp.int32)
    total_rows = I2_DEV * N_CUTS

    def step(acc, device):
        start = device * TILE_DEV
        vals = lax.dynamic_slice_in_dim(tile_vals, start, TILE_DEV, 0)
        counts = lax.dynamic_slice_in_dim(tile_count, start, TILE_DEV, 0)
        dests = lax.dynamic_slice_in_dim(tile_dest, start, TILE_DEV, 0)[:, 0]
        rows_in = lax.dynamic_slice_in_dim(tile_row, start, TILE_DEV, 0)
        blocks = lax.dynamic_slice_in_dim(tile_block, start, TILE_DEV, 0)
        firsts = lax.dynamic_slice_in_dim(tile_first, start, TILE_DEV, 0)
        masked = jnp.where(positions[None, :] < counts[:, None], vals, jnp.zeros_like(vals))
        fib = device % N_FIBER
        third = lax.dynamic_slice_in_dim(factor_three, fib * (KB_DEV * FIBER), KB_DEV * FIBER, 0)
        third = third.reshape(KB_DEV, FIBER, R3)
        picked = third[blocks].astype(jnp.float32)
        proj = jnp.einsum('tk,tkr->tr', masked.astype(jnp.float32), picked)
        first_rows = lax.dynamic_slice_in_dim(factor_one, device * I1_DEV, I1_DEV, 0)[firsts].astype(jnp.float32)
        kron = (first_rows[:, :, None] * proj[:, None, :]).reshape(TILE_DEV, R1 * R3)
        target = (dests * I2_DEV + rows_in).astype(jnp.int32)
        return acc + jax.ops.segment_sum(kron, target, num_segments=total_rows), None

    start_acc = jnp.zeros((total_rows, R1 * R3), jnp.float32)
    rows, _ = lax.scan(step, start_acc, jnp.arange(N_CUTS * N_FIBER, dtype=jnp.int32))
    ttmc = rows.astype(jnp.bfloat16)
    gram = lax.dot_general(ttmc, factor_two, (((0,), (0,)), ((), ())), preferred_element_type=jnp.float32)
    gram_b = gram.astype(jnp.bfloat16)
    projected = jnp.dot(ttmc, gram_b, preferred_element_type=jnp.float32) / 32.0
    return ttmc, projected
```

```python
import functools

import jax
import jax.numpy as jnp
from jax import lax
from jax.experimental import pallas as pl
from jax.experimental.pallas import tpu as pltpu
from jax.sharding import PartitionSpec as P

FIBER = 128
I2_DEV = 1024
CHUNK = 512
PARTS = 4
MESH = pl.DeviceIdType.MESH
NT = (((1,), (1,)), ((), ()))


def onehot(count, row, dtype=jnp.bfloat16):
    spots = lax.broadcasted_iota(jnp.int32, (count, row.shape[1]), 0).astype(row.dtype)
    return jnp.where(spots == row, 1.0, 0.0).astype(dtype)


def project_tiles(values, block_ids, factor_three):
    r3 = factor_three.shape[1]
    blocks = factor_three.shape[0] // FIBER
    table = factor_three.reshape(blocks, FIBER, r3).transpose(1, 0, 2).reshape(FIBER, blocks * r3)
    every = lax.dot_general(
        table, values, (((0,), (1,)), ((), ())), preferred_element_type=jnp.float32
    ).reshape(blocks, r3, values.shape[0])
    pick = (block_ids[None, :] == jnp.arange(blocks, dtype=jnp.int32)[:, None]).astype(jnp.float32)
    return jnp.sum(every * pick[:, None, :], axis=0)


def kernel(
    nc,
    nf,
    proj_ref,
    dest_ref,
    row_ref,
    first_ref,
    f1_ref,
    f2_ref,
    ttmc_ref,
    out_ref,
    data,
    member,
    slots,
    masked,
    send,
    got,
    kh,
    kl,
    acc,
    sib,
    xrecv,
    gram,
    grecv,
    gown,
    gall,
    gfull,
    a2a_send,
    a2a_recv,
    sib_send,
    sib_recv,
    x_send,
    x_recv,
    g_send,
    g_recv,
    b_send,
    b_recv,
):
    tiles = proj_ref.shape[1]
    r3 = proj_ref.shape[0]
    r1 = f1_ref.shape[0]
    r2 = f2_ref.shape[0]
    feats = data.shape[0]
    cap = tiles // nf
    br = f2_ref.shape[1]
    chunks = tiles // CHUNK
    width = r1 * r3
    nx = nc // 2
    ndev = nc * nf
    pieces = gram.shape[0]
    stride = ndev // pieces
    lanes = width // 128
    part = width // PARTS
    q = lax.axis_index("cuts")
    f = lax.axis_index("fiber")
    x = q // 2
    c = q % 2
    me = q * nf + f

    barrier = pltpu.get_barrier_semaphore()

    @pl.loop(1, ndev)
    def _(k):
        other = lax.rem(me + k, ndev)
        pl.semaphore_signal(
            barrier, inc=1, device_id=(other // nf, lax.rem(other, nf)), device_id_type=MESH
        )

    groups = lax.broadcasted_iota(jnp.int32, (nf, tiles), 0)
    owner = row_ref[...] // br
    member[...] = jnp.where(groups == owner, 1.0, 0.0)
    stacked = jnp.concatenate(
        [member[:, k * CHUNK : (k + 1) * CHUNK] for k in range(chunks)], axis=0
    )
    early = lax.broadcasted_iota(jnp.int32, (CHUNK, CHUNK), 0)
    late = lax.broadcasted_iota(jnp.int32, (CHUNK, CHUNK), 1)
    before = jnp.dot(
        stacked.astype(jnp.bfloat16),
        jnp.where(early < late, 1.0, 0.0).astype(jnp.bfloat16),
        preferred_element_type=jnp.float32,
    )
    carry = jnp.zeros((nf, 1), jnp.float32)
    for k in range(chunks):
        cols = slice(k * CHUNK, (k + 1) * CHUNK)
        mem = member[:, cols]
        rank = jnp.sum(mem * (before[k * nf : (k + 1) * nf] + carry), axis=0, keepdims=True)
        carry = carry + jnp.sum(mem, axis=1, keepdims=True)
        slots[:, cols] = onehot(cap, rank)
        value = proj_ref[:, cols]
        high = value.astype(jnp.bfloat16)
        data[0:r3, cols] = high
        data[r3 : 2 * r3, cols] = (value - high.astype(jnp.float32)).astype(jnp.bfloat16)
        data[2 * r3 : 2 * r3 + r1, cols] = jnp.dot(
            f1_ref[...],
            onehot(f1_ref.shape[1], first_ref[:, cols]),
            preferred_element_type=jnp.float32,
        ).astype(jnp.bfloat16)
        kind = lax.broadcasted_iota(jnp.int32, (16, CHUNK), 0)
        rows = row_ref[:, cols]
        marks = jnp.where(kind == 0, dest_ref[:, cols], jnp.where(kind == 1, rows % br, 0))
        data[2 * r3 + r1 :, cols] = marks.astype(jnp.float32).astype(jnp.bfloat16)

    def a2a_copy(j):
        to = lax.rem(f + j, nf)
        return pltpu.make_async_remote_copy(
            src_ref=send.at[j],
            dst_ref=got.at[j],
            send_sem=a2a_send.at[j],
            recv_sem=a2a_recv.at[j],
            device_id=(q, to),
            device_id_type=MESH,
        )

    def place(first_step):
        for half in range(2):
            group = lax.rem(f + first_step + half, nf)
            masked[half * feats : (half + 1) * feats, :] = data[...] * member[
                pl.ds(group, 1), :
            ].astype(jnp.bfloat16)
        return lax.dot_general(
            masked[...], slots[...], NT, preferred_element_type=jnp.float32
        ).astype(jnp.bfloat16)

    pl.semaphore_wait(barrier, ndev - 1)

    @pl.loop(0, nf // 2)
    def _(pair):
        j = 2 * pair + 1
        placed = place(j)
        send[j] = placed[:feats]
        a2a_copy(j).start()

        @pl.when(pair < nf // 2 - 1)
        def _():
            send[j + 1] = placed[feats:]
            a2a_copy(j + 1).start()

        @pl.when(pair == nf // 2 - 1)
        def _():
            got[0] = placed[feats:]

    def target(j, xs):
        marks = got[j, 2 * r3 + r1 :, :].astype(jnp.float32)
        key = (marks[0:1] - (2 * xs).astype(jnp.float32)) * br + marks[1:2]
        return onehot(2 * br, key)

    def add(slot, rows, total, fresh):
        for half in range(2):
            new = total[:, half * br : (half + 1) * br]
            if fresh:
                acc[slot, half, rows, :] = new
            else:
                acc[slot, half, rows, :] += new

    def sib_copy(slot, k):
        rows = pl.ds(k * part, part)
        return pltpu.make_async_remote_copy(
            src_ref=acc.at[slot, 1 - c, rows],
            dst_ref=sib.at[slot, rows],
            send_sem=sib_send.at[slot, k],
            recv_sem=sib_recv.at[slot, k],
            device_id=(x * 2 + 1 - c, f),
            device_id_type=MESH,
        )

    def x_copy(slot, k):
        rows = pl.ds(k * part, part)
        return pltpu.make_async_remote_copy(
            src_ref=acc.at[slot, c, rows],
            dst_ref=xrecv.at[slot, rows],
            send_sem=x_send.at[slot, k],
            recv_sem=x_recv.at[slot, k],
            device_id=(lax.rem(x + slot, nx) * 2 + c, f),
            device_id_type=MESH,
        )

    per = part // r3
    first_slot = 1 % nx

    def arrive(j, fresh):
        sel = target(j, lax.rem(x + first_slot, nx))
        value = got[j, 0:r3, :].astype(jnp.float32) + got[j, r3 : 2 * r3, :].astype(jnp.float32)
        fr = got[j, 2 * r3 : 2 * r3 + r1, :].astype(jnp.float32)
        for k in range(PARTS):
            rows = pl.ds(k * part, part)
            prod = jnp.concatenate(
                [fr[k * per + i : k * per + i + 1] * value for i in range(per)], axis=0
            )
            high = prod.astype(jnp.bfloat16)
            low = (prod - high.astype(jnp.float32)).astype(jnp.bfloat16)
            kh[j, rows, :] = high
            kl[j, rows, :] = low
            total = lax.dot_general(
                high, sel, NT, preferred_element_type=jnp.float32
            ) + lax.dot_general(low, sel, NT, preferred_element_type=jnp.float32)
            add(first_slot, rows, total, fresh)

    arrive(0, True)

    @pl.loop(1, nf)
    def _(j):
        a2a_copy(j).wait()
        arrive(j, False)

    def exchange(slot):
        for k in range(PARTS):
            sib_copy(slot, k).start()

    def forward(slot):
        for k in range(PARTS):
            rows = pl.ds(k * part, part)
            sib_copy(slot, k).wait()
            acc[slot, c, rows, :] += sib[slot, rows, :]
            if slot:
                x_copy(slot, k).start()

    def again(slot):
        @pl.loop(0, PARTS)
        def _(k):
            rows = pl.ds(pl.multiple_of(k * part, part), part)
            for j in range(nf):
                sel = target(j, lax.rem(x + slot, nx))
                total = lax.dot_general(
                    kh[j, rows, :], sel, NT, preferred_element_type=jnp.float32
                ) + lax.dot_general(kl[j, rows, :], sel, NT, preferred_element_type=jnp.float32)
                add(slot, rows, total, j == 0)

    exchange(first_slot)
    forward(first_slot)
    for slot in list(range(2, nx)) + ([0] if nx > 1 else []):
        again(slot)
        exchange(slot)
        forward(slot)

    for k in range(PARTS):
        rows = pl.ds(k * part, part)
        for slot in range(1, nx):
            x_copy(slot, k).wait()
        total = acc[0, c, rows, :]
        for slot in range(1, nx):
            total = total + xrecv[slot, rows, :]
        ttmc_ref[:, k * part : (k + 1) * part] = total.T.astype(jnp.bfloat16)

    ttmc = ttmc_ref[...]
    local = jnp.dot(f2_ref[...], ttmc, preferred_element_type=jnp.float32)
    for p in range(pieces):
        a, b = p // lanes, p % lanes
        gram[p] = local[a * 8 : (a + 1) * 8, b * 128 : (b + 1) * 128]

    def gram_copy(p):
        to = p * stride
        return pltpu.make_async_remote_copy(
            src_ref=gram.at[p],
            dst_ref=grecv.at[me],
            send_sem=g_send,
            recv_sem=g_recv,
            device_id=(to // nf, lax.rem(to, nf)),
            device_id_type=MESH,
        )

    def back_copy(k):
        to = lax.rem(me + k, ndev)
        return pltpu.make_async_remote_copy(
            src_ref=gown,
            dst_ref=gall.at[me // stride],
            send_sem=b_send,
            recv_sem=b_recv,
            device_id=(to // nf, lax.rem(to, nf)),
            device_id_type=MESH,
        )

    def drain(ref, count, sem):
        pltpu.make_async_copy(ref.at[pl.ds(0, count)], ref.at[pl.ds(0, count)], sem).wait()

    mine = me // stride
    owns = lax.rem(me, stride) == 0

    @pl.loop(0, pieces)
    def _(k):
        p = lax.rem(mine + k, pieces)

        @pl.when(p * stride != me)
        def _():
            gram_copy(p).start()

    @pl.when(owns)
    def _():
        grecv[me] = gram[mine]
        drain(grecv, ndev - 1, g_recv)
        gown[...] = jnp.sum(grecv[...], axis=0)
        gall[mine] = gown[...]

        @pl.loop(1, ndev)
        def _(k):
            back_copy(k).start()

        drain(gall, pieces - 1, b_recv)

    @pl.when(jnp.logical_not(owns))
    def _():
        drain(gall, pieces, b_recv)

    for p in range(pieces):
        a, b = p // lanes, p % lanes
        gfull[a * 8 : (a + 1) * 8, b * 128 : (b + 1) * 128] = gall[p]
    out_ref[...] = lax.dot_general(
        ttmc, gfull[...].astype(jnp.bfloat16), NT, preferred_element_type=jnp.float32
    ) / 32.0

    @pl.when(owns)
    def _():
        drain(gram, pieces - 1, g_send)
        drain(grecv, ndev - 1, b_send)

    @pl.when(jnp.logical_not(owns))
    def _():
        drain(gram, pieces, g_send)


def body(
    tile_vals,
    tile_count,
    tile_dest,
    tile_row,
    tile_block,
    tile_first,
    factor_one,
    factor_three,
    factor_two,
):
    nc = lax.axis_size("cuts")
    nf = lax.axis_size("fiber")
    tiles = tile_vals.shape[0]
    r1, r2, r3 = factor_one.shape[1], factor_two.shape[1], factor_three.shape[1]
    br = I2_DEV // nf
    cap = tiles // nf
    width = r1 * r3
    nx = nc // 2
    feats = 2 * r3 + r1 + 16
    pieces = (r2 // 8) * (width // 128)
    positions = jnp.arange(FIBER, dtype=jnp.int32)
    masked = jnp.where(
        positions[None, :] < tile_count[:, None], tile_vals, jnp.zeros_like(tile_vals)
    )
    proj = project_tiles(masked, tile_block, factor_three)
    vmem = pl.BlockSpec(memory_space=pltpu.VMEM)
    bf16, f32 = jnp.bfloat16, jnp.float32
    dma = pltpu.SemaphoreType.DMA
    return pl.pallas_call(
        functools.partial(kernel, nc, nf),
        out_shape=(
            jax.ShapeDtypeStruct((br, width), bf16),
            jax.ShapeDtypeStruct((br, r2), f32),
        ),
        in_specs=[vmem] * 6,
        out_specs=(vmem, vmem),
        scratch_shapes=[
            pltpu.VMEM((feats, tiles), bf16),
            pltpu.VMEM((nf, tiles), f32),
            pltpu.VMEM((cap, tiles), bf16),
            pltpu.VMEM((2 * feats, tiles), bf16),
            pltpu.VMEM((nf, feats, cap), bf16),
            pltpu.VMEM((nf, feats, cap), bf16),
            pltpu.VMEM((nf, width, cap), bf16),
            pltpu.VMEM((nf, width, cap), bf16),
            pltpu.VMEM((nx, 2, width, br), f32),
            pltpu.VMEM((nx, width, br), f32),
            pltpu.VMEM((nx, width, br), f32),
            pltpu.VMEM((pieces, 8, 128), f32),
            pltpu.VMEM((nc * nf, 8, 128), f32),
            pltpu.VMEM((8, 128), f32),
            pltpu.VMEM((pieces, 8, 128), f32),
            pltpu.VMEM((r2, width), f32),
            dma((nf,)),
            dma((nf,)),
            dma((nx, PARTS)),
            dma((nx, PARTS)),
            dma((nx, PARTS)),
            dma((nx, PARTS)),
            dma,
            dma,
            dma,
            dma,
        ],
        compiler_params=pltpu.CompilerParams(
            collective_id=0, has_side_effects=True, vmem_limit_bytes=60 * 1024 * 1024
        ),
    )(
        proj,
        tile_dest.reshape(1, tiles),
        tile_row.reshape(1, tiles),
        tile_first.reshape(1, tiles),
        factor_one.T,
        factor_two.T,
    )


def solution(mesh):
    in_specs = (
        P(("cuts", "fiber"), None),
        P(("cuts", "fiber")),
        P(("cuts", "fiber"), None),
        P(("cuts", "fiber")),
        P(("cuts", "fiber")),
        P(("cuts", "fiber")),
        P(("cuts", "fiber"), None),
        P("fiber", None),
        P(("cuts", "fiber"), None),
    )
    out_specs = (P(("cuts", "fiber"), None), P(("cuts", "fiber"), None))
    return jax.shard_map(body, mesh=mesh, in_specs=in_specs, out_specs=out_specs, check_vma=False)
```

```python
import functools

import jax
import jax.numpy as jnp
from jax import lax
from jax.experimental import pallas as pl
from jax.experimental.pallas import tpu as pltpu
from jax.sharding import PartitionSpec as P

FIBER = 128
I2_DEV = 1024
CHUNK = 512
PARTS = 4
MESH = pl.DeviceIdType.MESH
NT = (((1,), (1,)), ((), ()))


def onehot(count, row, dtype=jnp.bfloat16):
    spots = lax.broadcasted_iota(jnp.int32, (count, row.shape[1]), 0).astype(row.dtype)
    return jnp.where(spots == row, 1.0, 0.0).astype(dtype)


def project_tiles(values, block_ids, factor_three):
    r3 = factor_three.shape[1]
    blocks = factor_three.shape[0] // FIBER
    table = factor_three.reshape(blocks, FIBER, r3).transpose(1, 0, 2).reshape(FIBER, blocks * r3)
    every = lax.dot_general(
        table, values, (((0,), (1,)), ((), ())), preferred_element_type=jnp.float32
    ).reshape(blocks, r3, values.shape[0])
    pick = (block_ids[None, :] == jnp.arange(blocks, dtype=jnp.int32)[:, None]).astype(jnp.float32)
    return jnp.sum(every * pick[:, None, :], axis=0)


def kernel(
    nc,
    nf,
    proj_ref,
    dest_ref,
    row_ref,
    first_ref,
    f1_ref,
    f2_ref,
    ttmc_ref,
    out_ref,
    data,
    member,
    slots,
    masked,
    send,
    send_key,
    got,
    got_key,
    got_f1,
    acc,
    sib,
    gram,
    grecv,
    gown,
    gall,
    gfull,
    a2a_send,
    a2a_recv,
    x_send,
    x_recv,
    sib_send,
    sib_recv,
    g_send,
    g_recv,
    b_send,
    b_recv,
):
    tiles = proj_ref.shape[1]
    r3 = proj_ref.shape[0]
    r1, i1 = f1_ref.shape
    feats = data.shape[0]
    cap = tiles // nf
    br = f2_ref.shape[1]
    chunks = tiles // CHUNK
    width = r1 * r3
    nx = nc // 2
    ndev = nc * nf
    pieces = gram.shape[0]
    stride = ndev // pieces
    lanes = width // 128
    part = width // PARTS
    q = lax.axis_index("cuts")
    f = lax.axis_index("fiber")
    x = q // 2
    c = q % 2
    me = q * nf + f

    barrier = pltpu.get_barrier_semaphore()

    @pl.loop(1, ndev)
    def _(k):
        other = lax.rem(me + k, ndev)
        pl.semaphore_signal(
            barrier, inc=1, device_id=(other // nf, lax.rem(other, nf)), device_id_type=MESH
        )

    def a2a_copy(what, j):
        source = (send.at[j], send_key.at[j], f1_ref)[what]
        place_there = (got, got_key, got_f1)[what].at[0, j]
        return pltpu.make_async_remote_copy(
            src_ref=source,
            dst_ref=place_there,
            send_sem=a2a_send.at[what, j],
            recv_sem=a2a_recv.at[what, j],
            device_id=(q, lax.rem(f + j, nf)),
            device_id_type=MESH,
        )

    def x_copy(what, dx, j):
        where = (got, got_key, got_f1)[what]
        return pltpu.make_async_remote_copy(
            src_ref=where.at[0, j],
            dst_ref=where.at[dx, j],
            send_sem=x_send.at[what, dx, j],
            recv_sem=x_recv.at[what, dx, j],
            device_id=(lax.rem(x + dx, nx) * 2 + c, f),
            device_id_type=MESH,
        )

    groups = lax.broadcasted_iota(jnp.int32, (nf, tiles), 0)
    owner = row_ref[...] // br
    member[...] = jnp.where(groups == owner, 1.0, 0.0)
    got_f1[0, 0] = f1_ref[...]
    acc[...] = jnp.zeros_like(acc)
    stacked = jnp.concatenate(
        [member[:, k * CHUNK : (k + 1) * CHUNK] for k in range(chunks)], axis=0
    )
    early = lax.broadcasted_iota(jnp.int32, (CHUNK, CHUNK), 0)
    late = lax.broadcasted_iota(jnp.int32, (CHUNK, CHUNK), 1)
    before = jnp.dot(
        stacked.astype(jnp.bfloat16),
        jnp.where(early < late, 1.0, 0.0).astype(jnp.bfloat16),
        preferred_element_type=jnp.float32,
    )
    pl.semaphore_wait(barrier, ndev - 1)

    @pl.loop(1, nf)
    def _(j):
        a2a_copy(2, j).start()

    carry = jnp.zeros((nf, 1), jnp.float32)
    for k in range(chunks):
        cols = slice(k * CHUNK, (k + 1) * CHUNK)
        mem = member[:, cols]
        rank = jnp.sum(mem * (before[k * nf : (k + 1) * nf] + carry), axis=0, keepdims=True)
        carry = carry + jnp.sum(mem, axis=1, keepdims=True)
        slots[:, cols] = onehot(cap, rank)
        value = proj_ref[:, cols]
        high = value.astype(jnp.bfloat16)
        data[0:r3, cols] = high
        data[r3 : 2 * r3, cols] = (value - high.astype(jnp.float32)).astype(jnp.bfloat16)
        kind = lax.broadcasted_iota(jnp.int32, (16, CHUNK), 0)
        marks = jnp.where(
            kind == 0,
            dest_ref[:, cols],
            jnp.where(
                kind == 1,
                row_ref[:, cols] % br,
                jnp.where(kind == 2, first_ref[:, cols], 0),
            ),
        )
        data[2 * r3 :, cols] = marks.astype(jnp.float32).astype(jnp.bfloat16)

    @pl.loop(0, nf // 2)
    def _(pair):
        for half in range(2):
            group = lax.rem(f + nf // 2 + 2 * pair + half, nf)
            masked[half * feats : (half + 1) * feats, :] = data[...] * member[
                pl.ds(group, 1), :
            ].astype(jnp.bfloat16)
        placed = lax.dot_general(
            masked[...], slots[...], NT, preferred_element_type=jnp.float32
        )
        for half in range(2):
            j = lax.rem(nf // 2 + 2 * pair + half, nf)
            block = placed[half * feats : (half + 1) * feats]
            values = block[: 2 * r3].astype(jnp.bfloat16)
            marks = block[2 * r3 : 2 * r3 + 3]
            key = (marks[0:1] * br + marks[1:2]) * i1 + marks[2:3]

            def leave():
                send[j] = values
                send_key[j] = key
                a2a_copy(0, j).start()
                a2a_copy(1, j).start()

            def stay():
                got[0, 0] = values
                got_key[0, 0] = key

            if half:
                leave()
            else:
                pl.when(j != 0)(leave)
                pl.when(j == 0)(stay)

    per = part // r3

    def arrive(dx, j):
        key = got_key[dx, j]
        target = jnp.floor(key * (1.0 / i1))
        fr = jnp.dot(
            got_f1[dx, j], onehot(i1, key - target * i1), preferred_element_type=jnp.float32
        )
        sel = onehot(2 * br, target - (2 * x * br).astype(jnp.float32))
        value = got[dx, j, 0:r3, :].astype(jnp.float32) + got[dx, j, r3:, :].astype(jnp.float32)
        for k in range(PARTS):
            rows = pl.ds(k * part, part)
            prod = jnp.concatenate(
                [fr[k * per + i : k * per + i + 1] * value for i in range(per)], axis=0
            )
            high = prod.astype(jnp.bfloat16)
            low = (prod - high.astype(jnp.float32)).astype(jnp.bfloat16)
            total = lax.dot_general(
                high, sel, NT, preferred_element_type=jnp.float32
            ) + lax.dot_general(low, sel, NT, preferred_element_type=jnp.float32)
            for half in range(2):
                acc[half, rows, :] += total[:, half * br : (half + 1) * br]

    def turn(i):
        j = lax.rem(i + nf // 2 - 1 + i // (nf // 2 + 1), nf)
        return j * (1 - (nf - i) // nf)

    @pl.loop(0, nf + 1)
    def _(i):
        @pl.when(i < nf)
        def _():
            j = turn(i)

            @pl.when(i > 0)
            def _():
                for what in (2, 0, 1):
                    a2a_copy(what, j).wait()

            for dx in range(1, nx):
                for what in (2, 0, 1):
                    x_copy(what, dx, j).start()
            arrive(0, j)

        @pl.when(i > 0)
        def _():
            j = turn(i - 1)
            for dx in range(1, nx):
                for what in (2, 0, 1):
                    x_copy(what, dx, j).wait()
                arrive(dx, j)

    def sib_copy(k):
        rows = pl.ds(k * part, part)
        return pltpu.make_async_remote_copy(
            src_ref=acc.at[1 - c, rows],
            dst_ref=sib.at[rows],
            send_sem=sib_send.at[k],
            recv_sem=sib_recv.at[k],
            device_id=(x * 2 + 1 - c, f),
            device_id_type=MESH,
        )

    for k in range(PARTS):
        sib_copy(k).start()
    for k in range(PARTS):
        rows = pl.ds(k * part, part)
        sib_copy(k).wait()
        total = acc[c, rows, :] + sib[rows, :]
        ttmc_ref[:, k * part : (k + 1) * part] = total.T.astype(jnp.bfloat16)

    ttmc = ttmc_ref[...]
    local = jnp.dot(f2_ref[...], ttmc, preferred_element_type=jnp.float32)
    for p in range(pieces):
        a, b = p // lanes, p % lanes
        gram[p] = local[a * 8 : (a + 1) * 8, b * 128 : (b + 1) * 128]

    def gram_copy(p):
        to = p * stride
        return pltpu.make_async_remote_copy(
            src_ref=gram.at[p],
            dst_ref=grecv.at[me],
            send_sem=g_send,
            recv_sem=g_recv,
            device_id=(to // nf, lax.rem(to, nf)),
            device_id_type=MESH,
        )

    def back_copy(k):
        to = lax.rem(me + k, ndev)
        return pltpu.make_async_remote_copy(
            src_ref=gown,
            dst_ref=gall.at[me // stride],
            send_sem=b_send,
            recv_sem=b_recv,
            device_id=(to // nf, lax.rem(to, nf)),
            device_id_type=MESH,
        )

    def drain(ref, count, sem):
        pltpu.make_async_copy(ref.at[pl.ds(0, count)], ref.at[pl.ds(0, count)], sem).wait()

    mine = me // stride
    owns = lax.rem(me, stride) == 0

    @pl.loop(0, pieces)
    def _(k):
        p = lax.rem(mine + k, pieces)

        @pl.when(p * stride != me)
        def _():
            gram_copy(p).start()

    @pl.when(owns)
    def _():
        grecv[me] = gram[mine]
        drain(grecv, ndev - 1, g_recv)
        gown[...] = jnp.sum(grecv[...], axis=0)
        gall[mine] = gown[...]

        @pl.loop(1, ndev)
        def _(k):
            back_copy(k).start()

        drain(gall, pieces - 1, b_recv)

    @pl.when(jnp.logical_not(owns))
    def _():
        drain(gall, pieces, b_recv)

    for p in range(pieces):
        a, b = p // lanes, p % lanes
        gfull[a * 8 : (a + 1) * 8, b * 128 : (b + 1) * 128] = gall[p]
    out_ref[...] = lax.dot_general(
        ttmc, gfull[...].astype(jnp.bfloat16), NT, preferred_element_type=jnp.float32
    ) / 32.0

    @pl.when(owns)
    def _():
        drain(gram, pieces - 1, g_send)
        drain(grecv, ndev - 1, b_send)

    @pl.when(jnp.logical_not(owns))
    def _():
        drain(gram, pieces, g_send)


def body(
    tile_vals,
    tile_count,
    tile_dest,
    tile_row,
    tile_block,
    tile_first,
    factor_one,
    factor_three,
    factor_two,
):
    nc = lax.axis_size("cuts")
    nf = lax.axis_size("fiber")
    tiles = tile_vals.shape[0]
    r1, r2, r3 = factor_one.shape[1], factor_two.shape[1], factor_three.shape[1]
    br = I2_DEV // nf
    cap = tiles // nf
    width = r1 * r3
    nx = nc // 2
    i1 = factor_one.shape[0]
    feats = 2 * r3 + 16
    pieces = (r2 // 8) * (width // 128)
    positions = jnp.arange(FIBER, dtype=jnp.int32)
    masked = jnp.where(
        positions[None, :] < tile_count[:, None], tile_vals, jnp.zeros_like(tile_vals)
    )
    proj = project_tiles(masked, tile_block, factor_three)
    vmem = pl.BlockSpec(memory_space=pltpu.VMEM)
    bf16, f32 = jnp.bfloat16, jnp.float32
    dma = pltpu.SemaphoreType.DMA
    return pl.pallas_call(
        functools.partial(kernel, nc, nf),
        out_shape=(
            jax.ShapeDtypeStruct((br, width), bf16),
            jax.ShapeDtypeStruct((br, r2), f32),
        ),
        in_specs=[vmem] * 6,
        out_specs=(vmem, vmem),
        scratch_shapes=[
            pltpu.VMEM((feats, tiles), bf16),
            pltpu.VMEM((nf, tiles), f32),
            pltpu.VMEM((cap, tiles), bf16),
            pltpu.VMEM((2 * feats, tiles), bf16),
            pltpu.VMEM((nf, 2 * r3, cap), bf16),
            pltpu.VMEM((nf, 1, cap), f32),
            pltpu.VMEM((nx, nf, 2 * r3, cap), bf16),
            pltpu.VMEM((nx, nf, 1, cap), f32),
            pltpu.VMEM((nx, nf, r1, i1), bf16),
            pltpu.VMEM((2, width, br), f32),
            pltpu.VMEM((width, br), f32),
            pltpu.VMEM((pieces, 8, 128), f32),
            pltpu.VMEM((nc * nf, 8, 128), f32),
            pltpu.VMEM((8, 128), f32),
            pltpu.VMEM((pieces, 8, 128), f32),
            pltpu.VMEM((r2, width), f32),
            dma((3, nf)),
            dma((3, nf)),
            dma((3, nx, nf)),
            dma((3, nx, nf)),
            dma((PARTS,)),
            dma((PARTS,)),
            dma,
            dma,
            dma,
            dma,
        ],
        compiler_params=pltpu.CompilerParams(
            collective_id=0, has_side_effects=True, vmem_limit_bytes=60 * 1024 * 1024
        ),
    )(
        proj,
        tile_dest.reshape(1, tiles),
        tile_row.reshape(1, tiles),
        tile_first.reshape(1, tiles),
        factor_one.T,
        factor_two.T,
    )


def solution(mesh):
    in_specs = (
        P(("cuts", "fiber"), None),
        P(("cuts", "fiber")),
        P(("cuts", "fiber"), None),
        P(("cuts", "fiber")),
        P(("cuts", "fiber")),
        P(("cuts", "fiber")),
        P(("cuts", "fiber"), None),
        P("fiber", None),
        P(("cuts", "fiber"), None),
    )
    out_specs = (P(("cuts", "fiber"), None), P(("cuts", "fiber"), None))
    return jax.shard_map(body, mesh=mesh, in_specs=in_specs, out_specs=out_specs, check_vma=False)
```

```python
import functools

import jax
import jax.numpy as jnp
from jax import lax
from jax.experimental import pallas as pl
from jax.experimental.pallas import tpu as pltpu
from jax.sharding import PartitionSpec as P

FIBER = 128
I2_DEV = 1024
CHUNK = 512
PARTS = 4
MESH = pl.DeviceIdType.MESH
NT = (((1,), (1,)), ((), ()))


def onehot(count, row, dtype=jnp.bfloat16):
    spots = lax.broadcasted_iota(jnp.int32, (count, row.shape[1]), 0).astype(row.dtype)
    return jnp.where(spots == row, 1.0, 0.0).astype(dtype)


def project_tiles(values, block_ids, factor_three):
    r3 = factor_three.shape[1]
    blocks = factor_three.shape[0] // FIBER
    table = factor_three.reshape(blocks, FIBER, r3).transpose(1, 0, 2).reshape(FIBER, blocks * r3)
    every = lax.dot_general(
        table, values, (((0,), (1,)), ((), ())), preferred_element_type=jnp.float32
    ).reshape(blocks, r3, values.shape[0])
    pick = (block_ids[None, :] == jnp.arange(blocks, dtype=jnp.int32)[:, None]).astype(jnp.float32)
    return jnp.sum(every * pick[:, None, :], axis=0)


def kernel(
    nc,
    nf,
    proj_ref,
    dest_ref,
    row_ref,
    first_ref,
    f1_ref,
    f2_ref,
    ttmc_ref,
    out_ref,
    data,
    member,
    slots,
    masked,
    send,
    send_key,
    got,
    got_key,
    got_f1,
    acc,
    sib,
    gram,
    grecv,
    gown,
    gall,
    gfull,
    a2a_send,
    a2a_recv,
    x_send,
    x_recv,
    sib_send,
    sib_recv,
    g_send,
    g_recv,
    b_send,
    b_recv,
):
    tiles = proj_ref.shape[1]
    r3 = proj_ref.shape[0]
    r1, i1 = f1_ref.shape
    feats = data.shape[0]
    cap = tiles // nf
    br = f2_ref.shape[1]
    chunks = tiles // CHUNK
    width = r1 * r3
    nx = nc // 2
    ndev = nc * nf
    pieces = gram.shape[0]
    stride = ndev // pieces
    lanes = width // 128
    part = width // PARTS
    q = lax.axis_index("cuts")
    f = lax.axis_index("fiber")
    x = q // 2
    c = q % 2
    me = q * nf + f

    barrier = pltpu.get_barrier_semaphore()

    @pl.loop(1, ndev)
    def _(k):
        other = lax.rem(me + k, ndev)
        pl.semaphore_signal(
            barrier, inc=1, device_id=(other // nf, lax.rem(other, nf)), device_id_type=MESH
        )

    def a2a_copy(what, j):
        source = (send.at[j], send_key.at[j], f1_ref)[what]
        place_there = (got, got_key, got_f1)[what].at[0, j]
        return pltpu.make_async_remote_copy(
            src_ref=source,
            dst_ref=place_there,
            send_sem=a2a_send.at[what, j],
            recv_sem=a2a_recv.at[what, j],
            device_id=(q, lax.rem(f + j, nf)),
            device_id_type=MESH,
        )

    def x_copy(what, dx, j):
        where = (got, got_key, got_f1)[what]
        return pltpu.make_async_remote_copy(
            src_ref=where.at[0, j],
            dst_ref=where.at[dx, j],
            send_sem=x_send.at[what, dx, j],
            recv_sem=x_recv.at[what, dx, j],
            device_id=(lax.rem(x + dx, nx) * 2 + c, f),
            device_id_type=MESH,
        )

    groups = lax.broadcasted_iota(jnp.int32, (nf, tiles), 0)
    owner = row_ref[...] // br
    member[...] = jnp.where(groups == owner, 1.0, 0.0)
    got_f1[0, 0] = f1_ref[...]
    acc[...] = jnp.zeros_like(acc)
    stacked = jnp.concatenate(
        [member[:, k * CHUNK : (k + 1) * CHUNK] for k in range(chunks)], axis=0
    )
    early = lax.broadcasted_iota(jnp.int32, (CHUNK, CHUNK), 0)
    late = lax.broadcasted_iota(jnp.int32, (CHUNK, CHUNK), 1)
    before = jnp.dot(
        stacked.astype(jnp.bfloat16),
        jnp.where(early < late, 1.0, 0.0).astype(jnp.bfloat16),
        preferred_element_type=jnp.float32,
    )
    pl.semaphore_wait(barrier, ndev - 1)

    @pl.loop(1, nf)
    def _(j):
        a2a_copy(2, j).start()

    carry = jnp.zeros((nf, 1), jnp.float32)
    for k in range(chunks):
        cols = slice(k * CHUNK, (k + 1) * CHUNK)
        mem = member[:, cols]
        rank = jnp.sum(mem * (before[k * nf : (k + 1) * nf] + carry), axis=0, keepdims=True)
        carry = carry + jnp.sum(mem, axis=1, keepdims=True)
        slots[:, cols] = onehot(cap, rank)
        value = proj_ref[:, cols]
        high = value.astype(jnp.bfloat16)
        data[0:r3, cols] = high
        data[r3 : 2 * r3, cols] = (value - high.astype(jnp.float32)).astype(jnp.bfloat16)
        kind = lax.broadcasted_iota(jnp.int32, (16, CHUNK), 0)
        marks = jnp.where(
            kind == 0,
            dest_ref[:, cols],
            jnp.where(
                kind == 1,
                row_ref[:, cols] % br,
                jnp.where(kind == 2, first_ref[:, cols], 0),
            ),
        )
        data[2 * r3 :, cols] = marks.astype(jnp.float32).astype(jnp.bfloat16)

    def step_of(pair):
        late = (pair + nf // 2 - 1) // (nf // 2)
        return late * (2 + lax.rem(2 * (pair - 1) + nf // 2 - 2 + nf - 2, nf - 2))

    @pl.loop(0, nf // 2)
    def _(pair):
        for half in range(2):
            group = lax.rem(f + step_of(pair) + half, nf)
            masked[half * feats : (half + 1) * feats, :] = data[...] * member[
                pl.ds(group, 1), :
            ].astype(jnp.bfloat16)
        placed = lax.dot_general(
            masked[...], slots[...], NT, preferred_element_type=jnp.float32
        )
        for half in range(2):
            j = step_of(pair) + half
            block = placed[half * feats : (half + 1) * feats]
            values = block[: 2 * r3].astype(jnp.bfloat16)
            marks = block[2 * r3 : 2 * r3 + 3]
            key = (marks[0:1] * br + marks[1:2]) * i1 + marks[2:3]

            def leave():
                send[j] = values
                send_key[j] = key
                a2a_copy(0, j).start()
                a2a_copy(1, j).start()

            def stay():
                got[0, 0] = values
                got_key[0, 0] = key
                for dx in range(1, nx):
                    for what in range(2):
                        x_copy(what, dx, 0).start()

            if half:
                leave()
            else:
                pl.when(j != 0)(leave)
                pl.when(j == 0)(stay)

    for dx in range(1, nx):
        x_copy(2, dx, 0).start()

    @pl.loop(1, nf)
    def _(j):
        a2a_copy(2, j).wait()
        for dx in range(1, nx):
            x_copy(2, dx, j).start()

    per = part // r3

    def arrive(dx, j):
        key = got_key[dx, j]
        target = jnp.floor(key * (1.0 / i1))
        fr = jnp.dot(
            got_f1[dx, j], onehot(i1, key - target * i1), preferred_element_type=jnp.float32
        )
        sel = onehot(2 * br, target - (2 * x * br).astype(jnp.float32))
        value = got[dx, j, 0:r3, :].astype(jnp.float32) + got[dx, j, r3:, :].astype(jnp.float32)
        for k in range(PARTS):
            rows = pl.ds(k * part, part)
            prod = jnp.concatenate(
                [fr[k * per + i : k * per + i + 1] * value for i in range(per)], axis=0
            )
            high = prod.astype(jnp.bfloat16)
            low = (prod - high.astype(jnp.float32)).astype(jnp.bfloat16)
            total = lax.dot_general(
                high, sel, NT, preferred_element_type=jnp.float32
            ) + lax.dot_general(low, sel, NT, preferred_element_type=jnp.float32)
            for half in range(2):
                acc[half, rows, :] += total[:, half * br : (half + 1) * br]

    def turn(i):
        return step_of(i // 2) + lax.rem(i, 2)

    @pl.loop(0, nf + 1)
    def _(i):
        @pl.when(i < nf)
        def _():
            j = turn(i)

            @pl.when(i > 0)
            def _():
                for what in range(2):
                    a2a_copy(what, j).wait()
                for dx in range(1, nx):
                    for what in range(2):
                        x_copy(what, dx, j).start()

            arrive(0, j)

        @pl.when(i > 0)
        def _():
            j = turn(i - 1)
            for dx in range(1, nx):
                for what in (2, 0, 1):
                    x_copy(what, dx, j).wait()
                arrive(dx, j)

    def sib_copy(k):
        rows = pl.ds(k * part, part)
        return pltpu.make_async_remote_copy(
            src_ref=acc.at[1 - c, rows],
            dst_ref=sib.at[rows],
            send_sem=sib_send.at[k],
            recv_sem=sib_recv.at[k],
            device_id=(x * 2 + 1 - c, f),
            device_id_type=MESH,
        )

    for k in range(PARTS):
        sib_copy(k).start()
    for k in range(PARTS):
        rows = pl.ds(k * part, part)
        sib_copy(k).wait()
        total = acc[c, rows, :] + sib[rows, :]
        ttmc_ref[:, k * part : (k + 1) * part] = total.T.astype(jnp.bfloat16)

    ttmc = ttmc_ref[...]
    local = jnp.dot(f2_ref[...], ttmc, preferred_element_type=jnp.float32)
    for p in range(pieces):
        a, b = p // lanes, p % lanes
        gram[p] = local[a * 8 : (a + 1) * 8, b * 128 : (b + 1) * 128]

    def gram_copy(p):
        to = p * stride
        return pltpu.make_async_remote_copy(
            src_ref=gram.at[p],
            dst_ref=grecv.at[me],
            send_sem=g_send,
            recv_sem=g_recv,
            device_id=(to // nf, lax.rem(to, nf)),
            device_id_type=MESH,
        )

    def back_copy(k):
        to = lax.rem(me + k, ndev)
        return pltpu.make_async_remote_copy(
            src_ref=gown,
            dst_ref=gall.at[me // stride],
            send_sem=b_send,
            recv_sem=b_recv,
            device_id=(to // nf, lax.rem(to, nf)),
            device_id_type=MESH,
        )

    def drain(ref, count, sem):
        pltpu.make_async_copy(ref.at[pl.ds(0, count)], ref.at[pl.ds(0, count)], sem).wait()

    mine = me // stride
    owns = lax.rem(me, stride) == 0

    @pl.loop(0, pieces)
    def _(k):
        p = lax.rem(mine + k, pieces)

        @pl.when(p * stride != me)
        def _():
            gram_copy(p).start()

    @pl.when(owns)
    def _():
        grecv[me] = gram[mine]
        drain(grecv, ndev - 1, g_recv)
        gown[...] = jnp.sum(grecv[...], axis=0)
        gall[mine] = gown[...]

        @pl.loop(1, ndev)
        def _(k):
            back_copy(k).start()

        drain(gall, pieces - 1, b_recv)

    @pl.when(jnp.logical_not(owns))
    def _():
        drain(gall, pieces, b_recv)

    for p in range(pieces):
        a, b = p // lanes, p % lanes
        gfull[a * 8 : (a + 1) * 8, b * 128 : (b + 1) * 128] = gall[p]
    out_ref[...] = lax.dot_general(
        gfull[...].astype(jnp.bfloat16), ttmc, NT, preferred_element_type=jnp.float32
    ) / 32.0

    @pl.when(owns)
    def _():
        drain(gram, pieces - 1, g_send)
        drain(grecv, ndev - 1, b_send)

    @pl.when(jnp.logical_not(owns))
    def _():
        drain(gram, pieces, g_send)


def body(
    tile_vals,
    tile_count,
    tile_dest,
    tile_row,
    tile_block,
    tile_first,
    factor_one,
    factor_three,
    factor_two,
):
    nc = lax.axis_size("cuts")
    nf = lax.axis_size("fiber")
    tiles = tile_vals.shape[0]
    r1, r2, r3 = factor_one.shape[1], factor_two.shape[1], factor_three.shape[1]
    br = I2_DEV // nf
    cap = tiles // nf
    width = r1 * r3
    nx = nc // 2
    i1 = factor_one.shape[0]
    feats = 2 * r3 + 16
    pieces = (r2 // 8) * (width // 128)
    positions = jnp.arange(FIBER, dtype=jnp.int32)
    masked = jnp.where(
        positions[None, :] < tile_count[:, None], tile_vals, jnp.zeros_like(tile_vals)
    )
    proj = project_tiles(masked, tile_block, factor_three)
    vmem = pl.BlockSpec(memory_space=pltpu.VMEM)
    bf16, f32 = jnp.bfloat16, jnp.float32
    dma = pltpu.SemaphoreType.DMA
    ttmc, projected = pl.pallas_call(
        functools.partial(kernel, nc, nf),
        out_shape=(
            jax.ShapeDtypeStruct((br, width), bf16),
            jax.ShapeDtypeStruct((r2, br), f32),
        ),
        in_specs=[vmem] * 6,
        out_specs=(vmem, vmem),
        scratch_shapes=[
            pltpu.VMEM((feats, tiles), bf16),
            pltpu.VMEM((nf, tiles), f32),
            pltpu.VMEM((cap, tiles), bf16),
            pltpu.VMEM((2 * feats, tiles), bf16),
            pltpu.VMEM((nf, 2 * r3, cap), bf16),
            pltpu.VMEM((nf, 1, cap), f32),
            pltpu.VMEM((nx, nf, 2 * r3, cap), bf16),
            pltpu.VMEM((nx, nf, 1, cap), f32),
            pltpu.VMEM((nx, nf, r1, i1), bf16),
            pltpu.VMEM((2, width, br), f32),
            pltpu.VMEM((width, br), f32),
            pltpu.VMEM((pieces, 8, 128), f32),
            pltpu.VMEM((nc * nf, 8, 128), f32),
            pltpu.VMEM((8, 128), f32),
            pltpu.VMEM((pieces, 8, 128), f32),
            pltpu.VMEM((r2, width), f32),
            dma((3, nf)),
            dma((3, nf)),
            dma((3, nx, nf)),
            dma((3, nx, nf)),
            dma((PARTS,)),
            dma((PARTS,)),
            dma,
            dma,
            dma,
            dma,
        ],
        compiler_params=pltpu.CompilerParams(
            collective_id=0, has_side_effects=True, vmem_limit_bytes=60 * 1024 * 1024
        ),
    )(
        proj,
        tile_dest.reshape(1, tiles),
        tile_row.reshape(1, tiles),
        tile_first.reshape(1, tiles),
        factor_one.T,
        factor_two.T,
    )
    return ttmc, projected.T


def solution(mesh):
    in_specs = (
        P(("cuts", "fiber"), None),
        P(("cuts", "fiber")),
        P(("cuts", "fiber"), None),
        P(("cuts", "fiber")),
        P(("cuts", "fiber")),
        P(("cuts", "fiber")),
        P(("cuts", "fiber"), None),
        P("fiber", None),
        P(("cuts", "fiber"), None),
    )
    out_specs = (P(("cuts", "fiber"), None), P(("cuts", "fiber"), None))
    return jax.shard_map(body, mesh=mesh, in_specs=in_specs, out_specs=out_specs, check_vma=False)
```
